512 devices in a mesh: expert: 8 (over z_hi, core), tensor: 16 (over y, z_lo), dp: 4 (over x).
Axes of the slice: x: 4, y: 8, z: 8 (z_hi: 4, z_lo: 2; z = z_hi * 2 + z_lo), core: 2. Of those that a mesh axis runs over, the one named last changes fastest.
Arguments:
- tokens: bfloat16 [3072, 3072], P(('expert', 'dp'), 'tensor'), may hold values from -6 to 6
- out_grad: bfloat16 [3072, 3072], P(('expert', 'dp'), 'tensor'), may hold values from -6 to 6
- gates: float32 [3072, 2], P(('expert', 'dp')), may hold values from 0.2 to 1
- expert_ids: int32 [3072, 2], P(('expert', 'dp')), may hold values from 0 to 7, all different within a row; in each aligned block of 96 rows (0 to 95, 96 to 191, ...) at most 42 rows name the same one
- w_gate_up: bfloat16 [8, 2, 3072, 8192], P('expert', None, 'dp', 'tensor'), may hold values from -0.109375 to 0.109375
- w_down: bfloat16 [8, 8192, 3072], P('expert', 'tensor', 'dp'), may hold values from -0.109375 to 0.109375
Outputs:
- input_grad: bfloat16 [3072, 3072], P(('expert', 'dp'), 'tensor')
The draws below stay inside these ranges and needn't reach their ends.
Inputs may be any that keep to these rules, and one draw needn't show every extreme that they name: `expert_ids`: the two experts of a row differ; among the rows of one device no expert is named more than 42 times.
All inputs are finite; a program needn't handle non-finite values.
Results may differ from the reference program's by a relative error of at most 0.019.
Values may be sent and summed in bfloat16 or wider, within the bound.
A program may use at most 64 MiB of HBM per device.

```python
import math
import jax
import jax.numpy as jnp
import numpy as np
from jax import lax

D = 3072
FF = 8192
EXPERTS = 8
TOK_DEV = 96
TOKENS = 3072
CAP = 42
FF_GROUP = 512


def shard_levels(own_key, extent, split, low, top_value):
    def one(dim, shards_of):
        heights = jax.random.uniform(jax.random.fold_in(jax.random.fold_in(own_key, 6), dim), (shards_of,), jnp.float32, low / len(split), top_value / len(split))
        return jnp.repeat(jnp.exp(heights), extent[dim] // shards_of).reshape((-1,) + (1,) * (len(extent) - dim - 1))

    loudness = one(*split[0])
    for cut in split[1:]:
        loudness = loudness * one(*cut)
    return loudness


def routed_block(key, own, number, rows, count, top, most, lean):
    ranking = jax.random.permutation(key, count)
    heavy_load, usual = load_shares(count, rows * top, most, lean, True), load_shares(count, rows * top, most, lean, False)
    places = jnp.arange(count)

    def named(lengths, offset_by):
        used = int((lengths > 0).sum())
        fixed = max(1, used // 4)
        passed = fixed + (places - fixed + offset_by * (used - fixed)) % max(1, count - fixed)
        return jnp.zeros((count,), jnp.int32).at[ranking[jnp.where(places < fixed, places, passed)]].set(jnp.asarray(lengths, jnp.int32))

    lengths = jnp.where(number % 4 == 0, named(heavy_load, number // 4), named(usual, number - number // 4 - 1))
    mixed = jax.random.permutation(jax.random.fold_in(own, 3), count)
    donor, receiver = mixed[0:count // 2 * 2:2], mixed[1:count // 2 * 2:2]
    room = jnp.minimum(lengths[donor] - 1, most - lengths[receiver]) // 2
    room = jnp.where((donor == ranking[0]) | (receiver == ranking[0]) | (lengths[receiver] == 0), 0, jnp.maximum(room, 0))
    passed = jax.random.randint(jax.random.fold_in(own, 4), (count // 2,), 0, 1 << 20) % (room + 1)
    lengths = lengths.at[donor].add(-passed).at[receiver].add(passed)
    items = jnp.searchsorted(jnp.cumsum(lengths), jnp.arange(rows * top), side="right").astype(jnp.int32)
    grid = items.reshape(top, rows).T
    grid = grid[jax.random.permutation(jax.random.fold_in(own, 1), rows)]
    offset_by = jax.random.randint(jax.random.fold_in(own, 2), (rows, 1), 0, top)
    return jnp.take_along_axis(grid, (jnp.arange(top)[None, :] + offset_by) % top, axis=1)


def load_shares(number_of, total, bound, skew, full):
    loads = [(1 << 20) // math.isqrt(standing ** skew) + 1 for standing in range(1, number_of + 1)]
    largest = bound if full else min(bound, max(-(-total // number_of), total * loads[0] // sum(loads)))
    least = 1 if total - largest >= number_of - 1 else 0
    given, surplus = [largest] + [least] * (number_of - 1), total - largest - least * (number_of - 1)
    while surplus > 0:
        movable = [i for i in range(1, number_of) if given[i] < largest] or [i for i in range(1, number_of) if given[i] < bound]
        pool, left = sum([loads[i] for i in movable]), surplus
        for i in movable:
            more = min(bound - given[i], max(1, left * loads[i] // pool), surplus)
            given[i] = given[i] + more
            surplus = surplus - more
    return np.array(given)


def noise(key, shape, spread, most, split=(), kind=jnp.bfloat16):
    result = jax.random.normal(key, shape, jnp.float32) * spread
    if len(split) > 0:
        result = shard_levels(key, shape, split, -0.22, 0.18) * result
    return jnp.clip(result, min=-most, max=most).astype(kind)


def setup_inputs(seed: int = 0) -> dict:
    seeds = jax.random.split(jax.random.key(seed), 7)
    tokens = noise(seeds[0], (TOKENS, D), 1.0, 6.0, ((0, 32), (1, 16)))
    out_grad = noise(seeds[1], (TOKENS, D), 1.0, 6.0, ((0, 32), (1, 16)))
    gates = jnp.clip(0.2 + 0.8 * jax.random.uniform(seeds[2], (TOKENS, 2), jnp.float32) ** shard_levels(seeds[2], (TOKENS, 2), ((0, 32),), -0.2, 0.2), 0.2, 1.0)
    expert_ids_keys = jax.random.split(jax.random.fold_in(seeds[3], 1), TOKENS // TOK_DEV)
    expert_ids_turns = jax.random.permutation(jax.random.fold_in(seeds[3], 3), TOKENS // TOK_DEV)
    expert_ids = jax.vmap(lambda own, number: routed_block(jax.random.fold_in(seeds[3], 2), own, number, TOK_DEV, EXPERTS, 2, CAP, 2))(expert_ids_keys, expert_ids_turns).reshape((TOKENS, 2))
    w_gate_up = noise(seeds[4], (EXPERTS, 2, D, FF), D ** -0.5, 0.109375, ((0, 8), (2, 4), (3, 16)))
    w_down = noise(seeds[5], (EXPERTS, FF, D), D ** -0.5, 0.109375, ((0, 8), (1, 16), (2, 4)))
    return dict(tokens=tokens, out_grad=out_grad, gates=gates, expert_ids=expert_ids, w_gate_up=w_gate_up, w_down=w_down)


def expert_rows(flat_ids, expert, limit):
    keyed = jnp.where(flat_ids == expert, 0, 1).astype(jnp.int32)
    order = jnp.argsort(keyed, stable=True)[:limit].astype(jnp.int32)
    return order, flat_ids[order] == expert


def reference(tokens, out_grad, gates, expert_ids, w_gate_up, w_down):
    limit = TOKENS // TOK_DEV * CAP
    flat_ids = expert_ids.reshape(-1)
    flat_gates = gates.reshape(-1)

    def per_expert(expert, total):
        order, valid = expert_rows(flat_ids, expert, limit)
        row_index = order // 2
        inputs = tokens[row_index]
        grads = out_grad[row_index]
        weights = lax.dynamic_index_in_dim(w_gate_up, expert, 0, keepdims=False)
        down = lax.dynamic_index_in_dim(w_down, expert, 0, keepdims=False)
        gate_pre = jnp.dot(inputs, weights[0], preferred_element_type=jnp.float32)
        up_pre = jnp.dot(inputs, weights[1], preferred_element_type=jnp.float32)
        hidden_grad = jnp.dot(grads, down.T, preferred_element_type=jnp.float32)
        sigma = jax.nn.sigmoid(gate_pre)
        up_grad = (hidden_grad * gate_pre * sigma).astype(jnp.bfloat16)
        gate_grad = (hidden_grad * up_pre * sigma * (1.0 + gate_pre * (1.0 - sigma))).astype(jnp.bfloat16)

        def add_group(group, summed):
            begin = (jnp.asarray(group) * FF_GROUP).astype(jnp.int32)
            part = jnp.dot(lax.dynamic_slice_in_dim(gate_grad, begin, FF_GROUP, 1),
                           lax.dynamic_slice_in_dim(weights[0], begin, FF_GROUP, 1).T,
                           preferred_element_type=jnp.float32)
            part = part + jnp.dot(lax.dynamic_slice_in_dim(up_grad, begin, FF_GROUP, 1),
                                  lax.dynamic_slice_in_dim(weights[1], begin, FF_GROUP, 1).T,
                                  preferred_element_type=jnp.float32)
            rounded = lax.optimization_barrier(part.astype(jnp.bfloat16))
            return summed + rounded.astype(jnp.float32)

        summed = lax.fori_loop(0, FF // FF_GROUP, add_group, jnp.zeros((limit, D), jnp.float32))
        returned = lax.optimization_barrier(summed.astype(jnp.bfloat16)).astype(jnp.float32)
        scale = jnp.where(valid, flat_gates[order], jnp.float32(0.0)).astype(jnp.float32)
        return total.at[row_index].add(returned * scale[:, None])

    total = lax.fori_loop(0, EXPERTS, per_expert, jnp.zeros((TOKENS, D), jnp.float32))
    return total.astype(jnp.bfloat16)
```

```python
import jax
import jax.numpy as jnp
from jax import lax
from jax.experimental import pallas as pl
from jax.experimental.pallas import tpu as pltpu
from jax.sharding import PartitionSpec as P

MESH = pl.DeviceIdType.MESH
EXPERTS = 8
SLOTS = 42
PAD = 48
WIDTH = 192
PAIR = 384
ROWS = 176
HALF = 1536
SLICE = 768
UNITS = 512
NEAR_RIGHT = 2
NEAR_LEFT = 2
BF = jnp.bfloat16
F32 = jnp.float32


def iota(shape, dim):
    return lax.broadcasted_iota(jnp.int32, shape, dim)


def dot(a, b, ca=1, cb=0):
    return lax.dot_general(a, b, (((ca,), (cb,)), ((), ())), preferred_element_type=F32)


def onehot(mask):
    return mask.astype(F32).astype(BF)


class Copies:
    def __init__(self, send, recv):
        self.send, self.recv = send, recv
        self.sends, self.recvs = 0, 0
        self.pending = []

    def slots(self, count):
        first = self.recvs
        self.recvs += count
        return first

    def make(self, src, dst, device, slot=None):
        if slot is None:
            slot = self.slots(1)
        copy = pltpu.make_async_remote_copy(
            src_ref=src,
            dst_ref=dst,
            send_sem=self.send.at[self.sends],
            recv_sem=self.recv.at[slot],
            device_id=device,
            device_id_type=MESH,
        )
        self.sends += 1
        return copy

    def go(self, src, dst, device, slot=None):
        copy = self.make(src, dst, device, slot)
        copy.start()
        self.pending.append(copy)
        return copy

    def arrived(self, ref, slot):
        pltpu.make_async_copy(ref, ref, self.recv.at[slot]).wait()


SENDS = 160
RECVS = 160


def kernel(
    tokens_ref, grads_ref, gates_ref, ids_ref, wgu_hbm, wd_hbm,
    result_ref,
    outgoing, arrived, block, xg, wgu, wd, part, part_out, part_in, gu, rows_out, rows_in,
    final, final_in, back_out, back, send_sem, recv_sem, local_sem,
):
    e = lax.axis_index("expert")
    t = lax.axis_index("tensor")
    x = lax.axis_index("dp")
    c = lax.rem(e, 2)
    y, z = lax.div(t, 2), lax.rem(t, 2)
    yq = lax.rem(y - 2 * c + 8, 8)
    xq = lax.rem(x - c + 4, 4)
    h = lax.div(xq, 2)
    odd = lax.rem(xq, 2)

    right = {"tensor": 2 * lax.rem(y + 1, 8) + z}
    left = {"tensor": 2 * lax.rem(y + 7, 8) + z}
    across = {"tensor": 2 * y + (1 - z)}
    weights_peer = {"dp": lax.rem(xq + 1 - 2 * odd + c, 4)}
    rows_peer = {"dp": lax.rem(3 - xq + c, 4)}

    def place(core):
        xs = lax.rem(x - core + 4, 4)
        ys = lax.rem(y - 2 * core + 8, 8)
        flip = lax.rem(lax.div(xs, 2) + lax.div(ys, 4), 2)
        x2 = xs + flip * (3 - 2 * xs)
        y2 = ys + flip * (7 - 2 * ys)
        return lax.rem(x2 + core, 4), lax.rem(y2 + 2 * core, 8), flip

    places = [place(0), place(1)]
    px, py, pflip = place(c)
    copies = Copies(send_sem, recv_sem)

    barrier = pltpu.get_barrier_semaphore()
    signals = 0
    for peer in (right, left, across, weights_peer, rows_peer):
        pl.semaphore_signal(barrier, inc=1, device_id=peer, device_id_type=MESH)
        signals += 1
    for other in range(EXPERTS):
        ox, oy, _ = places[other % 2]
        for side in range(2):
            pl.semaphore_signal(
                barrier, inc=1, device_id={"expert": other, "tensor": 2 * oy + side, "dp": ox}, device_id_type=MESH
            )
            pl.semaphore_signal(
                barrier, inc=1, device_id={"expert": other, "tensor": 2 * py + side, "dp": px}, device_id_type=MESH
            )
            signals += 2

    mine = pl.multiple_of(odd * SLICE, SLICE)
    own_gu = pltpu.make_async_copy(wgu_hbm.at[0], wgu.at[:, pl.ds(mine, SLICE), :], local_sem.at[0])
    own_d = pltpu.make_async_copy(wd_hbm.at[0], wd.at[:, pl.ds(mine, SLICE)], local_sem.at[1])
    own_gu.start()
    own_d.start()

    ids = ids_ref[...]
    count = ids.shape[0]
    lanes = iota((count, EXPERTS), 1)
    chosen = [(ids[:, k : k + 1] == lanes).astype(F32) for k in range(2)]
    earlier = onehot(iota((count, count), 1) < iota((count, count), 0))
    before = dot(earlier, (chosen[0] + chosen[1]).astype(BF))
    slot_of = before + (lanes * PAD).astype(F32)
    slot_lanes = iota((count, EXPERTS * PAD), 1)
    picks = []
    for k in range(2):
        target = jnp.sum(chosen[k] * slot_of, axis=1, keepdims=True).astype(jnp.int32)
        picks.append((target == slot_lanes).astype(F32))
    select = (picks[0] + picks[1]).astype(BF)
    for kind, source in enumerate((tokens_ref, grads_ref)):
        chosen_rows = dot(select, source[...], 0, 0).astype(BF)
        outgoing[kind] = chosen_rows.reshape(EXPERTS, PAD, WIDTH)

    pl.semaphore_wait(barrier, signals)

    base = copies.slots(2 * EXPERTS)
    to_self = []
    for other in range(EXPERTS):
        ox, oy, oflip = places[other % 2]
        for kind in range(2):
            target = {"expert": other, "tensor": 2 * oy + kind, "dp": ox}
            slot = base + 2 * e + z
            copy = copies.make(outgoing.at[kind, other], arrived.at[e, z], target, slot)
            stays = jnp.logical_and(jnp.logical_and(e == other, z == kind), oflip == 0)
            here = pltpu.make_async_copy(outgoing.at[kind, other], arrived.at[e, z], recv_sem.at[slot])
            pl.when(stays)(here.start)
            pl.when(jnp.logical_not(stays))(copy.start)
            to_self.append((stays, copy))

    w1 = copies.go(wgu_hbm.at[0], wgu.at[:, pl.ds(mine, SLICE), :], weights_peer)
    w2 = copies.go(wd_hbm.at[0], wd.at[:, pl.ds(mine, SLICE)], weights_peer)

    embed = [onehot(iota((WIDTH, PAIR), 1) == iota((WIDTH, PAIR), 0) + WIDTH * side) for side in range(2)]
    dense = iota((ROWS, 4 * PAD), 0)
    padded = dense + (PAD - SLOTS) * sum((dense >= SLOTS * n).astype(jnp.int32) for n in range(1, 4))
    pack = onehot(jnp.logical_and(padded == iota((ROWS, 4 * PAD), 1), dense < 4 * SLOTS))

    def holds(origin):
        r = lax.div(origin, 4)
        same = 1 - lax.rem(r + h, 2)
        source = origin + (1 - same) * (7 - 2 * origin)
        return r, source - 4 * h

    def spot(n, kind, origin):
        r, pair = holds(origin)
        return xg.at[n, kind, r, :, pl.ds(pl.multiple_of(pair * PAIR, PAIR), PAIR)]

    def repack(n):
        for side in range(2):
            for source in range(4):
                copies.arrived(arrived.at[4 * n + source, side], base + 2 * (4 * n + source) + side)
        wide = sum(dot(arrived[4 * n : 4 * n + 4, side].reshape(4 * PAD, WIDTH), embed[side]) for side in range(2))
        block[n] = dot(pack, wide.astype(BF)).astype(BF)

    def gather(n):
        here = pltpu.make_async_copy(block.at[n], spot(n, z, yq), local_sem.at[2 + n])
        here.start()
        swap = copies.go(block.at[n], spot(n, z, yq), across)
        moves = {}

        def origin(way, step):
            return lax.rem(yq - step + 8, 8) if way == 0 else lax.rem(yq + step, 8)

        def push(way, kind, step, source=None):
            side = z if kind == 0 else 1 - z
            ref = spot(n, side, origin(way, step - 1))
            moves[way, kind, step] = copies.go(source if source is not None else ref, ref, right if way == 0 else left)

        reach = {(0, 0): 4, (1, 0): 3, (0, 1): NEAR_RIGHT, (1, 1): NEAR_LEFT}
        far = []
        push(0, 0, 1, block.at[n])
        push(1, 0, 1, block.at[n])
        yield
        swap.wait_recv()
        push(0, 1, 1)
        push(1, 1, 1)
        yield
        for step in range(1, 5):
            for way in range(2):
                if step > reach[way, 0]:
                    continue
                moves[way, 0, step].wait_recv()
                if step < reach[way, 0]:
                    push(way, 0, step + 1)
                if step > reach[way, 1]:
                    ref = spot(n, z, origin(way, step))
                    far.append(copies.go(ref, ref, across))
            yield
            for way in range(2):
                if step > reach[way, 1]:
                    continue
                moves[way, 1, step].wait_recv()
                if step < reach[way, 1]:
                    push(way, 1, step + 1)
            yield
        for copy in far:
            copy.wait_recv()
        here.wait()

    exchange = {}

    def forward(n):
        for which in range(3):
            data = xg[n, 1 if which == 2 else 0].reshape(2 * ROWS, HALF)
            if which < 2:
                value = dot(data, wgu[which])
            else:
                value = dot(data, wd[...], 1, 1)
            part[n, which] = value
            part_out[n, which] = value.astype(BF)
            exchange[n, which] = copies.go(part_out.at[n, which], part_in.at[n, which], rows_peer)
            yield

    def middle(n):
        for which in range(3):
            exchange[n, which].wait_recv()
        for r in range(2):
            span = pl.ds(r * ROWS, ROWS)
            gate, up, hidden = (part[n, w, span, :] + part_in[n, w, span, :].astype(F32) for w in range(3))
            sigma = jax.nn.sigmoid(gate)
            gu[n, r, :, :UNITS] = (hidden * up * sigma * (1.0 + gate * (1.0 - sigma))).astype(BF)
            gu[n, r, :, UNITS:] = (hidden * gate * sigma).astype(BF)
            yield

    def backward(n):
        def product(away):
            r, pair = holds(lax.rem(yq + away + 8, 8))
            span = pl.ds(pl.multiple_of(pair * PAIR, PAIR), PAIR)
            value = dot(gu[n, r, :, :UNITS], wgu[0, span, :], 1, 1)
            value = value + dot(gu[n, r, :, UNITS:], wgu[1, span, :], 1, 1)
            return value

        moves = {}
        chains = ((0, right, (4, 3, 2, 1)), (4, left, (-3, -2, -1)))
        for step in range(4):
            for first, way, aways in chains:
                if step >= len(aways):
                    continue
                index = first + step
                value = product(aways[step])
                if step > 0:
                    moves[index - 1].wait_recv()
                    value = value + rows_in[n, index - 1].astype(F32)
                rows_out[n, index] = value.astype(BF)
                moves[index] = copies.go(rows_out.at[n, index], rows_in.at[n, index], way)
            yield
        value = product(0)
        for last in (6, 3):
            moves[last].wait_recv()
            value = value + rows_in[n, last].astype(F32)
        final[n] = value
        yield

    def run(*work):
        for steps in work:
            for _ in steps:
                pass

    def advance(steps, times=1):
        for _ in range(times):
            next(steps, None)

    repack(0)
    gather_a = gather(0)
    advance(gather_a)
    repack(1)
    gather_b = gather(1)
    advance(gather_a, 3)
    advance(gather_b)
    run(gather_a)
    own_gu.wait()
    own_d.wait()
    w1.wait_recv()
    w2.wait_recv()
    advance(gather_b)
    for _ in forward(0):
        advance(gather_b, 2)
    run(gather_b)
    run(forward(1))
    run(middle(0))
    run(backward(0))
    run(middle(1))
    run(backward(1))

    final_out = final_in.at[1]
    final_in[1] = final[1 - z].astype(BF)
    cross = copies.go(final_out, final_in.at[0], across)
    cross.wait_recv()
    total = (final[z] + final_in[0].astype(F32)).astype(BF)
    unpacked = dot(pack, total, 0, 0).astype(BF)
    for side in range(2):
        back_out[side] = dot(unpacked, embed[side], 1, 1).astype(BF).reshape(4, PAD, WIDTH)

    base_back = copies.slots(EXPERTS)
    for source in range(4):
        for side in range(2):
            owner = 4 * z + source
            slot = base_back + e
            copy = copies.make(
                back_out.at[side, source], back.at[e], {"expert": owner, "tensor": 2 * py + side, "dp": px}, slot
            )
            stays = jnp.logical_and(jnp.logical_and(e == owner, z == side), pflip == 0)
            here = pltpu.make_async_copy(back_out.at[side, source], back.at[e], recv_sem.at[slot])
            pl.when(stays)(here.start)
            pl.when(jnp.logical_not(stays))(copy.start)
            to_self.append((stays, copy))
    for other in range(EXPERTS):
        copies.arrived(back.at[other], base_back + other)

    returned = back[...].reshape(EXPERTS * PAD, WIDTH)
    gates = gates_ref[...]
    total = jnp.zeros((count, WIDTH), F32)
    for k in range(2):
        total = total + gates[:, k : k + 1] * dot(picks[k].astype(BF), returned)
    result_ref[...] = total.astype(BF)

    for copy in copies.pending:
        copy.wait_send()
    for stays, copy in to_self:
        pl.when(jnp.logical_not(stays))(copy.wait_send)
    assert copies.sends <= SENDS and copies.recvs <= RECVS


def body(tokens, out_grad, gates, expert_ids, w_gate_up, w_down):
    vmem = pl.BlockSpec(memory_space=pltpu.VMEM)
    hbm = pl.BlockSpec(memory_space=pl.ANY)
    return pl.pallas_call(
        kernel,
        out_shape=jax.ShapeDtypeStruct(tokens.shape, BF),
        in_specs=[vmem, vmem, vmem, vmem, hbm, hbm],
        out_specs=vmem,
        scratch_shapes=[
            pltpu.VMEM((2, EXPERTS, PAD, WIDTH), BF),
            pltpu.VMEM((EXPERTS, 2, PAD, WIDTH), BF),
            pltpu.VMEM((2, ROWS, PAIR), BF),
            pltpu.VMEM((2, 2, 2, ROWS, HALF), BF),
            pltpu.VMEM((2, HALF, UNITS), BF),
            pltpu.VMEM((UNITS, HALF), BF),
            pltpu.VMEM((2, 3, 2 * ROWS, UNITS), F32),
            pltpu.VMEM((2, 3, 2 * ROWS, UNITS), BF),
            pltpu.VMEM((2, 3, 2 * ROWS, UNITS), BF),
            pltpu.VMEM((2, 2, ROWS, 2 * UNITS), BF),
            pltpu.VMEM((2, 7, ROWS, PAIR), BF),
            pltpu.VMEM((2, 7, ROWS, PAIR), BF),
            pltpu.VMEM((2, ROWS, PAIR), F32),
            pltpu.VMEM((2, ROWS, PAIR), BF),
            pltpu.VMEM((2, 4, PAD, WIDTH), BF),
            pltpu.VMEM((EXPERTS, PAD, WIDTH), BF),
            pltpu.SemaphoreType.DMA((SENDS,)),
            pltpu.SemaphoreType.DMA((RECVS,)),
            pltpu.SemaphoreType.DMA((4,)),
        ],
        compiler_params=pltpu.CompilerParams(
            collective_id=0, has_side_effects=True, vmem_limit_bytes=56 * 1024 * 1024
        ),
    )(tokens, out_grad, gates, expert_ids, w_gate_up, w_down)


def solution(mesh):
    return jax.shard_map(
        body,
        mesh=mesh,
        in_specs=(
            P(("expert", "dp"), "tensor"),
            P(("expert", "dp"), "tensor"),
            P(("expert", "dp"), None),
            P(("expert", "dp"), None),
            P("expert", None, "dp", "tensor"),
            P("expert", "tensor", "dp"),
        ),
        out_specs=P(("expert", "dp"), "tensor"),
        check_vma=False,
    )
```

```python
import jax
import jax.numpy as jnp
from jax import lax
from jax.experimental import pallas as pl
from jax.experimental.pallas import tpu as pltpu
from jax.sharding import PartitionSpec as P

MESH = pl.DeviceIdType.MESH
EXPERTS = 8
SLOTS = 42
PAD = 48
WIDTH = 192
PAIR = 384
ROWS = 176
HALF = 1536
SLICE = 768
UNITS = 512
NEAR_RIGHT = 1
NEAR_LEFT = 2
ORDER = (4, 5, 3, 2, 6, 1, 7, 0)
BF = jnp.bfloat16
F32 = jnp.float32


def iota(shape, dim):
    return lax.broadcasted_iota(jnp.int32, shape, dim)


def dot(a, b, ca=1, cb=0):
    return lax.dot_general(a, b, (((ca,), (cb,)), ((), ())), preferred_element_type=F32)


def onehot(mask):
    return mask.astype(F32).astype(BF)


class Copies:
    def __init__(self, send, recv):
        self.send, self.recv = send, recv
        self.sends, self.recvs = 0, 0
        self.pending = []

    def slots(self, count):
        first = self.recvs
        self.recvs += count
        return first

    def make(self, src, dst, device, slot=None):
        if slot is None:
            slot = self.slots(1)
        copy = pltpu.make_async_remote_copy(
            src_ref=src,
            dst_ref=dst,
            send_sem=self.send.at[self.sends],
            recv_sem=self.recv.at[slot],
            device_id=device,
            device_id_type=MESH,
        )
        self.sends += 1
        return copy

    def go(self, src, dst, device, slot=None):
        copy = self.make(src, dst, device, slot)
        copy.start()
        self.pending.append(copy)
        return copy

    def arrived(self, ref, slot):
        pltpu.make_async_copy(ref, ref, self.recv.at[slot]).wait()


SENDS = 160
RECVS = 160


def kernel(
    tokens_ref, grads_ref, gates_ref, ids_ref, wgu_hbm, wd_hbm,
    result_ref,
    outgoing, arrived, packed, block, xg, wgu, wd, part, part_out, part_in, gu, rows_out, rows_in,
    final, final_in, back_out, back, send_sem, recv_sem, local_sem,
):
    e = lax.axis_index("expert")
    t = lax.axis_index("tensor")
    x = lax.axis_index("dp")
    c = lax.rem(e, 2)
    y, z = lax.div(t, 2), lax.rem(t, 2)
    yq = lax.rem(y - 2 * c + 8, 8)
    xq = lax.rem(x - c + 4, 4)
    h = lax.div(xq, 2)
    odd = lax.rem(xq, 2)

    right = {"tensor": 2 * lax.rem(y + 1, 8) + z}
    left = {"tensor": 2 * lax.rem(y + 7, 8) + z}
    across = {"tensor": 2 * y + (1 - z)}
    weights_peer = {"dp": lax.rem(xq + 1 - 2 * odd + c, 4)}
    rows_peer = {"dp": lax.rem(3 - xq + c, 4)}

    def place(core):
        xs = lax.rem(x - core + 4, 4)
        ys = lax.rem(y - 2 * core + 8, 8)
        flip = lax.rem(lax.div(xs, 2) + lax.div(ys, 4), 2)
        x2 = xs + flip * (3 - 2 * xs)
        y2 = ys + flip * (6 + 2 * lax.rem(ys, 2) - 2 * ys)
        return lax.rem(x2 + core, 4), lax.rem(y2 + 2 * core, 8), flip

    px, py, pflip = place(c)
    mirror = {"tensor": 2 * py + z, "dp": px}
    copies = Copies(send_sem, recv_sem)

    barrier = pltpu.get_barrier_semaphore()
    signals = 0
    for peer in (right, left, across, weights_peer, rows_peer, mirror):
        pl.semaphore_signal(barrier, inc=1, device_id=peer, device_id_type=MESH)
        signals += 1
    for other in range(EXPERTS):
        for side in range(2):
            pl.semaphore_signal(
                barrier, inc=1, device_id={"expert": other, "tensor": 2 * y + side}, device_id_type=MESH
            )
            signals += 1

    mine = pl.multiple_of(odd * SLICE, SLICE)
    own_gu = pltpu.make_async_copy(wgu_hbm.at[0], wgu.at[:, pl.ds(mine, SLICE), :], local_sem.at[0])
    own_d = pltpu.make_async_copy(wd_hbm.at[0], wd.at[:, pl.ds(mine, SLICE)], local_sem.at[1])
    own_gu.start()
    own_d.start()

    ids = ids_ref[...]
    count = ids.shape[1]
    lines = iota((EXPERTS, count), 0)
    chosen = [(ids[k : k + 1, :] == lines).astype(F32) for k in range(2)]
    earlier = onehot(iota((count, count), 0) < iota((count, count), 1))
    before = dot((chosen[0] + chosen[1]).astype(BF), earlier)
    slot_of = before + (lines * PAD).astype(F32)
    slot_lines = iota((EXPERTS * PAD, count), 0)
    picks = []
    for k in range(2):
        target = jnp.sum(chosen[k] * slot_of, axis=0, keepdims=True).astype(jnp.int32)
        picks.append((target == slot_lines).astype(F32))
    select = (picks[0] + picks[1]).astype(BF)
    for kind, source in enumerate((tokens_ref, grads_ref)):
        chosen_rows = dot(select, source[...]).astype(BF)
        outgoing[kind] = chosen_rows.reshape(EXPERTS, PAD, WIDTH)

    pl.semaphore_wait(barrier, signals)

    base = copies.slots(2 * EXPERTS)
    to_self = []
    for turn in ORDER:
        other = lax.rem(e + turn, EXPERTS)
        for kind in range(2):
            target = {"expert": other, "tensor": 2 * y + kind}
            slot = base + 2 * e + z
            copy = copies.make(outgoing.at[kind, other], arrived.at[e, z], target, slot)
            if turn:
                copy.start()
                copies.pending.append(copy)
                continue
            stays = z == kind
            here = pltpu.make_async_copy(outgoing.at[kind, other], arrived.at[e, z], recv_sem.at[slot])
            pl.when(stays)(here.start)
            pl.when(jnp.logical_not(stays))(copy.start)
            to_self.append((stays, copy))

    w1 = copies.go(wgu_hbm.at[0], wgu.at[:, pl.ds(mine, SLICE), :], weights_peer)
    w2 = copies.go(wd_hbm.at[0], wd.at[:, pl.ds(mine, SLICE)], weights_peer)

    embed = [onehot(iota((WIDTH, PAIR), 1) == iota((WIDTH, PAIR), 0) + WIDTH * side) for side in range(2)]
    dense = iota((ROWS, 4 * PAD), 0)
    padded = dense + (PAD - SLOTS) * sum((dense >= SLOTS * n).astype(jnp.int32) for n in range(1, 4))
    pack = onehot(jnp.logical_and(padded == iota((ROWS, 4 * PAD), 1), dense < 4 * SLOTS))

    def holds(origin):
        r = lax.div(origin, 4)
        same = 1 - lax.rem(r + h, 2)
        source = origin + (1 - same) * (6 + 2 * lax.rem(origin, 2) - 2 * origin)
        return r, source - 4 * h

    def spot(n, kind, origin):
        r, pair = holds(origin)
        return xg.at[n, kind, r, :, pl.ds(pl.multiple_of(pair * PAIR, PAIR), PAIR)]

    def repack(n):
        for side in range(2):
            for source in range(4):
                copies.arrived(arrived.at[4 * n + source, side], base + 2 * (4 * n + source) + side)
        wide = sum(dot(arrived[4 * n : 4 * n + 4, side].reshape(4 * PAD, WIDTH), embed[side]) for side in range(2))
        packed[n] = dot(pack, wide.astype(BF)).astype(BF)
        copy = copies.make(packed.at[n], block.at[n], mirror)
        here = pltpu.make_async_copy(packed.at[n], block.at[n], recv_sem.at[copies.recvs - 1])
        pl.when(pflip == 0)(here.start)
        pl.when(pflip == 1)(copy.start)
        to_self.append((pflip == 0, copy))
        return here

    class Gather:
        reach = {(0, 0): 4, (1, 0): 3, (0, 1): NEAR_RIGHT, (1, 1): NEAR_LEFT}

        def __init__(self, n):
            self.n = n
            self.moves = {}
            self.far = []
            self.here = pltpu.make_async_copy(block.at[n], spot(n, z, yq), local_sem.at[2 + n])
            self.here.start()
            self.push(0, 0, 1, block.at[n])
            self.push(1, 0, 1, block.at[n])
            self.swap = copies.go(block.at[n], spot(n, z, yq), across)

        def origin(self, way, step):
            return lax.rem(yq - step + 8, 8) if way == 0 else lax.rem(yq + step, 8)

        def push(self, way, kind, step, source=None):
            side = z if kind == 0 else 1 - z
            ref = spot(self.n, side, self.origin(way, step - 1))
            self.moves[way, kind, step] = copies.go(ref if source is None else source, ref, right if way == 0 else left)

        def swapped(self):
            self.swap.wait_recv()
            self.push(0, 1, 1)
            self.push(1, 1, 1)

        def own(self, step):
            for way in range(2):
                if step <= self.reach[way, 0]:
                    self.moves[way, 0, step].wait_recv()
                    if step < self.reach[way, 0]:
                        self.push(way, 0, step + 1)
                    if step > self.reach[way, 1]:
                        ref = spot(self.n, z, self.origin(way, step))
                        self.far.append(copies.go(ref, ref, across))

        def other(self, step):
            for way in range(2):
                if step <= self.reach[way, 1]:
                    self.moves[way, 1, step].wait_recv()
                    if step < self.reach[way, 1]:
                        self.push(way, 1, step + 1)

        def finish(self):
            for copy in self.far:
                copy.wait_recv()
            self.here.wait()

    exchange = {}

    def forward(n):
        for which in range(3):
            data = xg[n, 1 if which == 2 else 0].reshape(2 * ROWS, HALF)
            if which < 2:
                value = dot(data, wgu[which])
            else:
                value = dot(data, wd[...], 1, 1)
            part[n, which] = value
            part_out[n, which] = value.astype(BF)
            exchange[n, which] = copies.go(part_out.at[n, which], part_in.at[n, which], rows_peer)
            yield

    def middle(n):
        for which in range(3):
            exchange[n, which].wait_recv()
        for r in range(2):
            span = pl.ds(r * ROWS, ROWS)
            gate, up, hidden = (part[n, w, span, :] + part_in[n, w, span, :].astype(F32) for w in range(3))
            sigma = jax.nn.sigmoid(gate)
            gu[n, r, :, :UNITS] = (hidden * up * sigma * (1.0 + gate * (1.0 - sigma))).astype(BF)
            gu[n, r, :, UNITS:] = (hidden * gate * sigma).astype(BF)
            yield

    def backward(n):
        def product(away):
            r, pair = holds(lax.rem(yq + away + 8, 8))
            span = pl.ds(pl.multiple_of(pair * PAIR, PAIR), PAIR)
            value = dot(gu[n, r, :, :UNITS], wgu[0, span, :], 1, 1)
            value = value + dot(gu[n, r, :, UNITS:], wgu[1, span, :], 1, 1)
            return value

        moves = {}
        chains = ((0, right, (4, 3, 2, 1)), (4, left, (-3, -2, -1)))
        for step in range(4):
            for first, way, aways in chains:
                if step >= len(aways):
                    continue
                index = first + step
                value = product(aways[step])
                if step > 0:
                    moves[index - 1].wait_recv()
                    value = value + rows_in[n, index - 1].astype(F32)
                rows_out[n, index] = value.astype(BF)
                moves[index] = copies.go(rows_out.at[n, index], rows_in.at[n, index], way)
            yield
        value = product(0)
        for last in (6, 3):
            moves[last].wait_recv()
            value = value + rows_in[n, last].astype(F32)
        final[n] = value
        yield

    def run(*work):
        for steps in work:
            for _ in steps:
                pass

    def advance(steps, times=1):
        for _ in range(times):
            next(steps, None)

    swap_a = repack(0)
    swap_b = repack(1)
    swap_a.wait()
    ga = Gather(0)
    swap_b.wait()
    gb = Gather(1)
    ga.own(1)
    ga.swapped()
    ga.own(2)
    ga.other(1)
    ga.own(3)
    gb.own(1)
    gb.swapped()
    ga.own(4)
    ga.other(2)
    gb.own(2)
    gb.other(1)
    ga.finish()
    own_gu.wait()
    own_d.wait()
    w1.wait_recv()
    w2.wait_recv()
    fa = forward(0)
    advance(fa)
    gb.own(3)
    gb.other(2)
    run(fa)
    gb.own(4)
    gb.finish()
    run(forward(1))
    run(middle(0))
    ba = backward(0)
    advance(ba, 3)
    run(middle(1))
    bb = backward(1)
    advance(bb)
    advance(ba)
    advance(bb)
    advance(ba)
    run(bb)

    final_out = final_in.at[1]
    final_in[1] = final[1 - z].astype(BF)
    cross = copies.go(final_out, final_in.at[0], across)
    cross.wait_recv()
    total = (final[z] + final_in[0].astype(F32)).astype(BF)
    unpacked = dot(pack, total, 0, 0).astype(BF)
    for side in range(2):
        back_out[side] = dot(unpacked, embed[side], 1, 1).astype(BF).reshape(4, PAD, WIDTH)

    base_back = copies.slots(EXPERTS)
    for turn in (2, 3, 1, 0):
        source = lax.rem(e + turn, 4)
        owner = 4 * z + source
        for side in range(2):
            slot = base_back + e
            copy = copies.make(
                back_out.at[side, source], back.at[e], {"expert": owner, "tensor": 2 * py + side, "dp": px}, slot
            )
            stays = jnp.logical_and(jnp.logical_and(e == owner, z == side), pflip == 0)
            here = pltpu.make_async_copy(back_out.at[side, source], back.at[e], recv_sem.at[slot])
            pl.when(stays)(here.start)
            pl.when(jnp.logical_not(stays))(copy.start)
            to_self.append((stays, copy))
    for other in range(EXPERTS):
        copies.arrived(back.at[other], base_back + other)

    returned = back[...].reshape(EXPERTS * PAD, WIDTH)
    gates = gates_ref[...]
    diagonal = iota((count, count), 0) == iota((count, count), 1)
    total = jnp.zeros((count, WIDTH), F32)
    for k in range(2):
        gate = jnp.sum(jnp.where(diagonal, gates[k : k + 1, :], 0.0), axis=1, keepdims=True)
        total = total + gate * dot(picks[k].astype(BF), returned, 0, 0)
    result_ref[...] = total.astype(BF)

    for copy in copies.pending:
        copy.wait_send()
    for stays, copy in to_self:
        pl.when(jnp.logical_not(stays))(copy.wait_send)
    assert copies.sends <= SENDS and copies.recvs <= RECVS


def body(tokens, out_grad, gates, expert_ids, w_gate_up, w_down):
    vmem = pl.BlockSpec(memory_space=pltpu.VMEM)
    hbm = pl.BlockSpec(memory_space=pl.ANY)
    return pl.pallas_call(
        kernel,
        out_shape=jax.ShapeDtypeStruct(tokens.shape, BF),
        in_specs=[vmem, vmem, vmem, vmem, hbm, hbm],
        out_specs=vmem,
        scratch_shapes=[
            pltpu.VMEM((2, EXPERTS, PAD, WIDTH), BF),
            pltpu.VMEM((EXPERTS, 2, PAD, WIDTH), BF),
            pltpu.VMEM((2, ROWS, PAIR), BF),
            pltpu.VMEM((2, ROWS, PAIR), BF),
            pltpu.VMEM((2, 2, 2, ROWS, HALF), BF),
            pltpu.VMEM((2, HALF, UNITS), BF),
            pltpu.VMEM((UNITS, HALF), BF),
            pltpu.VMEM((2, 3, 2 * ROWS, UNITS), F32),
            pltpu.VMEM((2, 3, 2 * ROWS, UNITS), BF),
            pltpu.VMEM((2, 3, 2 * ROWS, UNITS), BF),
            pltpu.VMEM((2, 2, ROWS, 2 * UNITS), BF),
            pltpu.VMEM((2, 7, ROWS, PAIR), BF),
            pltpu.VMEM((2, 7, ROWS, PAIR), BF),
            pltpu.VMEM((2, ROWS, PAIR), F32),
            pltpu.VMEM((2, ROWS, PAIR), BF),
            pltpu.VMEM((2, 4, PAD, WIDTH), BF),
            pltpu.VMEM((EXPERTS, PAD, WIDTH), BF),
            pltpu.SemaphoreType.DMA((SENDS,)),
            pltpu.SemaphoreType.DMA((RECVS,)),
            pltpu.SemaphoreType.DMA((4,)),
        ],
        compiler_params=pltpu.CompilerParams(
            collective_id=0, has_side_effects=True, vmem_limit_bytes=56 * 1024 * 1024
        ),
    )(tokens, out_grad, gates.T, expert_ids.T, w_gate_up, w_down)


def solution(mesh):
    return jax.shard_map(
        body,
        mesh=mesh,
        in_specs=(
            P(("expert", "dp"), "tensor"),
            P(("expert", "dp"), "tensor"),
            P(("expert", "dp"), None),
            P(("expert", "dp"), None),
            P("expert", None, "dp", "tensor"),
            P("expert", "tensor", "dp"),
        ),
        out_specs=P(("expert", "dp"), "tensor"),
        check_vma=False,
    )
```

```python
import jax
import jax.numpy as jnp
from jax import lax
from jax.experimental import pallas as pl
from jax.experimental.pallas import tpu as pltpu
from jax.sharding import PartitionSpec as P

MESH = pl.DeviceIdType.MESH
EXPERTS = 8
SLOTS = 42
PAD = 48
WIDTH = 192
PAIR = 384
ROWS = 176
HALF = 1536
SLICE = 768
UNITS = 512
NEAR_RIGHT = 1
NEAR_LEFT = 2
ORDER = (4, 5, 3, 2, 6, 1, 7, 0)
BF = jnp.bfloat16
F32 = jnp.float32


def iota(shape, dim):
    return lax.broadcasted_iota(jnp.int32, shape, dim)


def dot(a, b, ca=1, cb=0):
    return lax.dot_general(a, b, (((ca,), (cb,)), ((), ())), preferred_element_type=F32)


def onehot(mask):
    return mask.astype(F32).astype(BF)


class Copies:
    def __init__(self, send, recv):
        self.send, self.recv = send, recv
        self.sends, self.recvs = 0, 0
        self.pending = []

    def slots(self, count):
        first = self.recvs
        self.recvs += count
        return first

    def make(self, src, dst, device, slot=None):
        if slot is None:
            slot = self.slots(1)
        copy = pltpu.make_async_remote_copy(
            src_ref=src,
            dst_ref=dst,
            send_sem=self.send.at[self.sends],
            recv_sem=self.recv.at[slot],
            device_id=device,
            device_id_type=MESH,
        )
        self.sends += 1
        return copy

    def go(self, src, dst, device, slot=None):
        copy = self.make(src, dst, device, slot)
        copy.start()
        self.pending.append(copy)
        return copy

    def arrived(self, ref, slot):
        pltpu.make_async_copy(ref, ref, self.recv.at[slot]).wait()


SENDS = 160
RECVS = 160


def kernel(
    tokens_ref, grads_ref, gates_ref, ids_ref, wgu_hbm, wd_hbm,
    result_ref,
    outgoing, arrived, packed, block, xg, wgu, wd, part, part_out, part_in, gu, products, swapped,
    rows_out, rows_in, back_out, back, send_sem, recv_sem, local_sem,
):
    e = lax.axis_index("expert")
    t = lax.axis_index("tensor")
    x = lax.axis_index("dp")
    c = lax.rem(e, 2)
    y, z = lax.div(t, 2), lax.rem(t, 2)
    yq = lax.rem(y - 2 * c + 8, 8)
    xq = lax.rem(x - c + 4, 4)
    h = lax.div(xq, 2)
    odd = lax.rem(xq, 2)

    right = {"tensor": 2 * lax.rem(y + 1, 8) + z}
    left = {"tensor": 2 * lax.rem(y + 7, 8) + z}
    across = {"tensor": 2 * y + (1 - z)}
    weights_peer = {"dp": lax.rem(xq + 1 - 2 * odd + c, 4)}
    rows_peer = {"dp": lax.rem(3 - xq + c, 4)}

    def place(core):
        xs = lax.rem(x - core + 4, 4)
        ys = lax.rem(y - 2 * core + 8, 8)
        flip = lax.rem(lax.div(xs, 2) + lax.div(ys, 4), 2)
        x2 = xs + flip * (3 - 2 * xs)
        y2 = ys + flip * (6 + 2 * lax.rem(ys, 2) - 2 * ys)
        return lax.rem(x2 + core, 4), lax.rem(y2 + 2 * core, 8), flip

    px, py, pflip = place(c)
    mirror = {"tensor": 2 * py + z, "dp": px}
    copies = Copies(send_sem, recv_sem)

    barrier = pltpu.get_barrier_semaphore()
    signals = 0
    for peer in (right, left, across, weights_peer, rows_peer, mirror):
        pl.semaphore_signal(barrier, inc=1, device_id=peer, device_id_type=MESH)
        signals += 1
    for other in range(EXPERTS):
        for side in range(2):
            pl.semaphore_signal(
                barrier, inc=1, device_id={"expert": other, "tensor": 2 * y + side}, device_id_type=MESH
            )
            signals += 1

    mine = pl.multiple_of(odd * SLICE, SLICE)
    own_gu = pltpu.make_async_copy(wgu_hbm.at[0], wgu.at[:, pl.ds(mine, SLICE), :], local_sem.at[0])
    own_d = pltpu.make_async_copy(wd_hbm.at[0], wd.at[:, pl.ds(mine, SLICE)], local_sem.at[1])
    own_gu.start()
    own_d.start()

    ids = ids_ref[...]
    count = ids.shape[1]
    lines = iota((EXPERTS, count), 0)
    chosen = [(ids[k : k + 1, :] == lines).astype(F32) for k in range(2)]
    earlier = onehot(iota((count, count), 0) < iota((count, count), 1))
    before = dot((chosen[0] + chosen[1]).astype(BF), earlier)
    slot_of = before + (lines * PAD).astype(F32)
    slot_lines = iota((EXPERTS * PAD, count), 0)
    picks = []
    for k in range(2):
        target = jnp.sum(chosen[k] * slot_of, axis=0, keepdims=True).astype(jnp.int32)
        picks.append((target == slot_lines).astype(F32))
    select = (picks[0] + picks[1]).astype(BF)
    for kind, source in enumerate((tokens_ref, grads_ref)):
        chosen_rows = dot(select, source[...]).astype(BF)
        outgoing[kind] = chosen_rows.reshape(EXPERTS, PAD, WIDTH)

    pl.semaphore_wait(barrier, signals)

    base = copies.slots(2 * EXPERTS)
    to_self = []
    for turn in ORDER:
        other = lax.rem(e + turn, EXPERTS)
        for kind in range(2):
            target = {"expert": other, "tensor": 2 * y + kind}
            slot = base + 2 * e + z
            copy = copies.make(outgoing.at[kind, other], arrived.at[e, z], target, slot)
            if turn:
                copy.start()
                copies.pending.append(copy)
                continue
            stays = z == kind
            here = pltpu.make_async_copy(outgoing.at[kind, other], arrived.at[e, z], recv_sem.at[slot])
            pl.when(stays)(here.start)
            pl.when(jnp.logical_not(stays))(copy.start)
            to_self.append((stays, copy))

    w1 = copies.go(wgu_hbm.at[0], wgu.at[:, pl.ds(mine, SLICE), :], weights_peer)
    w2 = copies.go(wd_hbm.at[0], wd.at[:, pl.ds(mine, SLICE)], weights_peer)

    embed = [onehot(iota((WIDTH, PAIR), 1) == iota((WIDTH, PAIR), 0) + WIDTH * side) for side in range(2)]
    dense = iota((ROWS, 4 * PAD), 0)
    padded = dense + (PAD - SLOTS) * sum((dense >= SLOTS * n).astype(jnp.int32) for n in range(1, 4))
    pack = onehot(jnp.logical_and(padded == iota((ROWS, 4 * PAD), 1), dense < 4 * SLOTS))

    def holds(origin):
        r = lax.div(origin, 4)
        same = 1 - lax.rem(r + h, 2)
        source = origin + (1 - same) * (6 + 2 * lax.rem(origin, 2) - 2 * origin)
        return r, source - 4 * h

    def spot(n, kind, origin):
        r, pair = holds(origin)
        return xg.at[n, kind, r, :, pl.ds(pl.multiple_of(pair * PAIR, PAIR), PAIR)]

    def repack(n):
        for side in range(2):
            for source in range(4):
                copies.arrived(arrived.at[4 * n + source, side], base + 2 * (4 * n + source) + side)
        wide = sum(dot(arrived[4 * n : 4 * n + 4, side].reshape(4 * PAD, WIDTH), embed[side]) for side in range(2))
        packed[n] = dot(pack, wide.astype(BF)).astype(BF)
        copy = copies.make(packed.at[n], block.at[n], mirror)
        here = pltpu.make_async_copy(packed.at[n], block.at[n], recv_sem.at[copies.recvs - 1])
        pl.when(pflip == 0)(here.start)
        pl.when(pflip == 1)(copy.start)
        to_self.append((pflip == 0, copy))
        return here

    class Gather:
        reach = {(0, 0): 4, (1, 0): 3, (0, 1): NEAR_RIGHT, (1, 1): NEAR_LEFT}

        def __init__(self, n):
            self.n = n
            self.moves = {}
            self.far = []
            self.here = pltpu.make_async_copy(block.at[n], spot(n, z, yq), local_sem.at[2 + n])
            self.here.start()
            self.push(0, 0, 1, block.at[n])
            self.push(1, 0, 1, block.at[n])
            self.swap = copies.go(block.at[n], spot(n, z, yq), across)

        def origin(self, way, step):
            return lax.rem(yq - step + 8, 8) if way == 0 else lax.rem(yq + step, 8)

        def push(self, way, kind, step, source=None):
            side = z if kind == 0 else 1 - z
            ref = spot(self.n, side, self.origin(way, step - 1))
            self.moves[way, kind, step] = copies.go(ref if source is None else source, ref, right if way == 0 else left)

        def swapped(self):
            self.swap.wait_recv()
            self.push(0, 1, 1)
            self.push(1, 1, 1)

        def own(self, step):
            for way in range(2):
                if step <= self.reach[way, 0]:
                    self.moves[way, 0, step].wait_recv()
                    if step < self.reach[way, 0]:
                        self.push(way, 0, step + 1)
                    if step > self.reach[way, 1]:
                        ref = spot(self.n, z, self.origin(way, step))
                        self.far.append(copies.go(ref, ref, across))

        def other(self, step):
            for way in range(2):
                if step <= self.reach[way, 1]:
                    self.moves[way, 1, step].wait_recv()
                    if step < self.reach[way, 1]:
                        self.push(way, 1, step + 1)

        def finish(self):
            for copy in self.far:
                copy.wait_recv()
            self.here.wait()

    exchange = {}

    def forward(n):
        for which in range(3):
            data = xg[n, 1 if which == 2 else 0].reshape(2 * ROWS, HALF)
            if which < 2:
                value = dot(data, wgu[which])
            else:
                value = dot(data, wd[...], 1, 1)
            part[n, which] = value
            part_out[n, which] = value.astype(BF)
            exchange[n, which] = copies.go(part_out.at[n, which], part_in.at[n, which], rows_peer)
            yield

    def middle(n):
        for which in range(3):
            exchange[n, which].wait_recv()
        for r in range(2):
            span = pl.ds(r * ROWS, ROWS)
            gate, up, hidden = (part[n, w, span, :] + part_in[n, w, span, :].astype(F32) for w in range(3))
            sigma = jax.nn.sigmoid(gate)
            gate_grad = (hidden * up * sigma * (1.0 + gate * (1.0 - sigma))).astype(BF)
            up_grad = (hidden * gate * sigma).astype(BF)
            gu[n, r, :, :UNITS] = dot(pack, gate_grad, 0, 0).astype(BF)
            gu[n, r, :, UNITS:] = dot(pack, up_grad, 0, 0).astype(BF)
            yield

    back_base = copies.slots(EXPERTS)

    def backward(n):
        aways = (4, 3, 2, 1, -3, -2, -1, 0)
        swaps, moves = {}, {}

        def product(index):
            r, pair = holds(lax.rem(yq + aways[index] + 8, 8))
            span = pl.ds(pl.multiple_of(pair * PAIR, PAIR), PAIR)
            value = dot(gu[n, r, :, :UNITS], wgu[0, span, :], 1, 1)
            value = value + dot(gu[n, r, :, UNITS:], wgu[1, span, :], 1, 1)
            products[n, index] = value.astype(BF).reshape(2, 2 * PAD, PAIR)
            swaps[index] = copies.go(products.at[n, index, 1 - z], swapped.at[n, index], across)

        def mine(index):
            swaps[index].wait_recv()
            return products[n, index, z].astype(F32) + swapped[n, index].astype(F32)

        def link(index, way, first):
            value = mine(index)
            if not first:
                moves[index - 1].wait_recv()
                value = value + rows_in[n, index - 1].astype(F32)
            rows_out[n, index] = value.astype(BF)
            moves[index] = copies.go(rows_out.at[n, index], rows_in.at[n, index], way)

        for index in (0, 4, 1, 5):
            product(index)
        link(0, right, True)
        link(4, left, True)
        for index in (2, 6, 3, 7):
            product(index)
        yield
        link(1, right, False)
        link(5, left, False)
        yield
        link(2, right, False)
        link(6, left, False)
        yield
        link(3, right, False)
        yield
        value = mine(7)
        for last in (6, 3):
            moves[last].wait_recv()
            value = value + rows_in[n, last].astype(F32)
        total = value.astype(BF)
        for side in range(2):
            back_out[n, side] = dot(total, embed[side], 1, 1).astype(BF).reshape(2, PAD, WIDTH)
        for turn in range(2):
            source = lax.rem(e + turn, 2)
            owner = 4 * n + 2 * z + source
            for side in range(2):
                slot = back_base + e
                target = {"expert": owner, "tensor": 2 * py + side, "dp": px}
                copy = copies.make(back_out.at[n, side, source], back.at[e], target, slot)
                stays = jnp.logical_and(jnp.logical_and(e == owner, z == side), pflip == 0)
                here = pltpu.make_async_copy(back_out.at[n, side, source], back.at[e], recv_sem.at[slot])
                pl.when(stays)(here.start)
                pl.when(jnp.logical_not(stays))(copy.start)
                to_self.append((stays, copy))
        yield

    def run(*work):
        for steps in work:
            for _ in steps:
                pass

    def advance(steps, times=1):
        for _ in range(times):
            next(steps, None)

    swap_a = repack(0)
    swap_b = repack(1)
    swap_a.wait()
    ga = Gather(0)
    swap_b.wait()
    gb = Gather(1)
    ga.own(1)
    ga.swapped()
    ga.own(2)
    ga.other(1)
    ga.own(3)
    gb.own(1)
    gb.swapped()
    ga.own(4)
    ga.other(2)
    gb.own(2)
    gb.other(1)
    ga.finish()
    own_gu.wait()
    own_d.wait()
    w1.wait_recv()
    w2.wait_recv()
    fa = forward(0)
    advance(fa)
    gb.own(3)
    gb.other(2)
    run(fa)
    gb.own(4)
    gb.finish()
    run(forward(1))
    run(middle(0))
    ba = backward(0)
    advance(ba, 2)
    run(middle(1))
    bb = backward(1)
    for _ in range(3):
        advance(bb)
        advance(ba)
    run(bb)
    for other in range(EXPERTS):
        copies.arrived(back.at[other], back_base + other)

    returned = back[...].reshape(EXPERTS * PAD, WIDTH)
    gates = gates_ref[...]
    diagonal = iota((count, count), 0) == iota((count, count), 1)
    total = jnp.zeros((count, WIDTH), F32)
    for k in range(2):
        gate = jnp.sum(jnp.where(diagonal, gates[k : k + 1, :], 0.0), axis=1, keepdims=True)
        total = total + gate * dot(picks[k].astype(BF), returned, 0, 0)
    result_ref[...] = total.astype(BF)

    for copy in copies.pending:
        copy.wait_send()
    for stays, copy in to_self:
        pl.when(jnp.logical_not(stays))(copy.wait_send)
    assert copies.sends <= SENDS and copies.recvs <= RECVS


def body(tokens, out_grad, gates, expert_ids, w_gate_up, w_down):
    vmem = pl.BlockSpec(memory_space=pltpu.VMEM)
    hbm = pl.BlockSpec(memory_space=pl.ANY)
    return pl.pallas_call(
        kernel,
        out_shape=jax.ShapeDtypeStruct(tokens.shape, BF),
        in_specs=[vmem, vmem, vmem, vmem, hbm, hbm],
        out_specs=vmem,
        scratch_shapes=[
            pltpu.VMEM((2, EXPERTS, PAD, WIDTH), BF),
            pltpu.VMEM((EXPERTS, 2, PAD, WIDTH), BF),
            pltpu.VMEM((2, ROWS, PAIR), BF),
            pltpu.VMEM((2, ROWS, PAIR), BF),
            pltpu.VMEM((2, 2, 2, ROWS, HALF), BF),
            pltpu.VMEM((2, HALF, UNITS), BF),
            pltpu.VMEM((UNITS, HALF), BF),
            pltpu.VMEM((2, 3, 2 * ROWS, UNITS), F32),
            pltpu.VMEM((2, 3, 2 * ROWS, UNITS), BF),
            pltpu.VMEM((2, 3, 2 * ROWS, UNITS), BF),
            pltpu.VMEM((2, 2, 4 * PAD, 2 * UNITS), BF),
            pltpu.VMEM((2, 8, 2, 2 * PAD, PAIR), BF),
            pltpu.VMEM((2, 8, 2 * PAD, PAIR), BF),
            pltpu.VMEM((2, 7, 2 * PAD, PAIR), BF),
            pltpu.VMEM((2, 7, 2 * PAD, PAIR), BF),
            pltpu.VMEM((2, 2, 2, PAD, WIDTH), BF),
            pltpu.VMEM((EXPERTS, PAD, WIDTH), BF),
            pltpu.SemaphoreType.DMA((SENDS,)),
            pltpu.SemaphoreType.DMA((RECVS,)),
            pltpu.SemaphoreType.DMA((4,)),
        ],
        compiler_params=pltpu.CompilerParams(
            collective_id=0, has_side_effects=True, vmem_limit_bytes=56 * 1024 * 1024
        ),
    )(tokens, out_grad, gates.T, expert_ids.T, w_gate_up, w_down)


def solution(mesh):
    return jax.shard_map(
        body,
        mesh=mesh,
        in_specs=(
            P(("expert", "dp"), "tensor"),
            P(("expert", "dp"), "tensor"),
            P(("expert", "dp"), None),
            P(("expert", "dp"), None),
            P("expert", None, "dp", "tensor"),
            P("expert", "tensor", "dp"),
        ),
        out_specs=P(("expert", "dp"), "tensor"),
        check_vma=False,
    )
```

```python
import jax
import jax.numpy as jnp
from jax import lax
from jax.experimental import pallas as pl
from jax.experimental.pallas import tpu as pltpu
from jax.sharding import PartitionSpec as P

MESH = pl.DeviceIdType.MESH
EXPERTS = 8
SLOTS = 42
PAD = 48
WIDTH = 192
PAIR = 384
ROWS = 176
HALF = 1536
SLICE = 768
UNITS = 512
NEAR_RIGHT = 1
NEAR_LEFT = 1
ORDER = (4, 5, 3, 2, 6, 1, 7, 0)
BF = jnp.bfloat16
F32 = jnp.float32


def iota(shape, dim):
    return lax.broadcasted_iota(jnp.int32, shape, dim)


def dot(a, b, ca=1, cb=0):
    return lax.dot_general(a, b, (((ca,), (cb,)), ((), ())), preferred_element_type=F32)


def onehot(mask):
    return mask.astype(F32).astype(BF)


class Copies:
    def __init__(self, send, recv):
        self.send, self.recv = send, recv
        self.sends, self.recvs = 0, 0
        self.pending = []

    def slots(self, count):
        first = self.recvs
        self.recvs += count
        return first

    def make(self, src, dst, device, slot=None):
        if slot is None:
            slot = self.slots(1)
        copy = pltpu.make_async_remote_copy(
            src_ref=src,
            dst_ref=dst,
            send_sem=self.send.at[self.sends],
            recv_sem=self.recv.at[slot],
            device_id=device,
            device_id_type=MESH,
        )
        self.sends += 1
        return copy

    def go(self, src, dst, device, slot=None):
        copy = self.make(src, dst, device, slot)
        copy.start()
        self.pending.append(copy)
        return copy

    def arrived(self, ref, slot):
        pltpu.make_async_copy(ref, ref, self.recv.at[slot]).wait()


SENDS = 160
RECVS = 160


def kernel(
    tokens_hbm, grads_hbm, gates_hbm, ids_hbm, wgu_hbm, wd_hbm,
    result_ref,
    outgoing, arrived, packed, block, xg, wgu, wd, part, part_out, part_in, gu, products, swapped,
    rows_out, rows_in, back_out, back, tokens_ref, grads_ref, gates_ref, ids_ref, send_sem, recv_sem, local_sem,
):
    e = lax.axis_index("expert")
    t = lax.axis_index("tensor")
    x = lax.axis_index("dp")
    c = lax.rem(e, 2)
    y, z = lax.div(t, 2), lax.rem(t, 2)
    yq = lax.rem(y - 2 * c + 8, 8)
    xq = lax.rem(x - c + 4, 4)
    h = lax.div(xq, 2)
    odd = lax.rem(xq, 2)

    right = {"tensor": 2 * lax.rem(y + 1, 8) + z}
    left = {"tensor": 2 * lax.rem(y + 7, 8) + z}
    across = {"tensor": 2 * y + (1 - z)}
    weights_peer = {"dp": lax.rem(xq + 1 - 2 * odd + c, 4)}
    rows_peer = {"dp": lax.rem(3 - xq + c, 4)}

    def place(core):
        xs = lax.rem(x - core + 4, 4)
        ys = lax.rem(y - 2 * core + 8, 8)
        flip = lax.rem(lax.div(xs, 2) + lax.div(ys, 4), 2)
        x2 = xs + flip * (3 - 2 * xs)
        y2 = ys + flip * (6 + 2 * lax.rem(ys, 2) - 2 * ys)
        return lax.rem(x2 + core, 4), lax.rem(y2 + 2 * core, 8), flip

    px, py, pflip = place(c)
    mirror = {"tensor": 2 * py + z, "dp": px}
    copies = Copies(send_sem, recv_sem)

    barrier = pltpu.get_barrier_semaphore()
    signals = 0
    for peer in (right, left, across, weights_peer, rows_peer, mirror):
        pl.semaphore_signal(barrier, inc=1, device_id=peer, device_id_type=MESH)
        signals += 1
    for other in range(EXPERTS):
        for side in range(2):
            pl.semaphore_signal(
                barrier, inc=1, device_id={"expert": other, "tensor": 2 * y + side}, device_id_type=MESH
            )
            signals += 1

    loads = [
        pltpu.make_async_copy(source, target, local_sem.at[4 + i])
        for i, (source, target) in enumerate(
            ((ids_hbm, ids_ref), (tokens_hbm, tokens_ref), (grads_hbm, grads_ref), (gates_hbm, gates_ref))
        )
    ]
    for load in loads:
        load.start()
    mine = pl.multiple_of(odd * SLICE, SLICE)
    own_gu = pltpu.make_async_copy(wgu_hbm.at[0], wgu.at[:, pl.ds(mine, SLICE), :], local_sem.at[0])
    own_d = pltpu.make_async_copy(wd_hbm.at[0], wd.at[:, pl.ds(mine, SLICE)], local_sem.at[1])
    own_gu.start()
    own_d.start()

    for load in loads:
        load.wait()
    ids = ids_ref[...]
    count = ids.shape[1]
    lines = iota((EXPERTS, count), 0)
    chosen = [(ids[k : k + 1, :] == lines).astype(F32) for k in range(2)]
    earlier = onehot(iota((count, count), 0) < iota((count, count), 1))
    before = dot((chosen[0] + chosen[1]).astype(BF), earlier)
    slot_of = before + (lines * PAD).astype(F32)
    slot_lines = iota((EXPERTS * PAD, count), 0)
    picks = []
    for k in range(2):
        target = jnp.sum(chosen[k] * slot_of, axis=0, keepdims=True).astype(jnp.int32)
        picks.append((target == slot_lines).astype(F32))
    select = (picks[0] + picks[1]).astype(BF)
    for kind, source in enumerate((tokens_ref, grads_ref)):
        chosen_rows = dot(select, source[...]).astype(BF)
        outgoing[kind] = chosen_rows.reshape(EXPERTS, PAD, WIDTH)

    pl.semaphore_wait(barrier, signals)

    base = copies.slots(2 * EXPERTS)
    to_self = []
    for turn in ORDER:
        other = lax.rem(e + turn, EXPERTS)
        for kind in range(2):
            target = {"expert": other, "tensor": 2 * y + kind}
            slot = base + 2 * e + z
            copy = copies.make(outgoing.at[kind, other], arrived.at[e, z], target, slot)
            if turn:
                copy.start()
                copies.pending.append(copy)
                continue
            stays = z == kind
            here = pltpu.make_async_copy(outgoing.at[kind, other], arrived.at[e, z], recv_sem.at[slot])
            pl.when(stays)(here.start)
            pl.when(jnp.logical_not(stays))(copy.start)
            to_self.append((stays, copy))

    w1 = copies.go(wgu_hbm.at[0], wgu.at[:, pl.ds(mine, SLICE), :], weights_peer)
    w2 = copies.go(wd_hbm.at[0], wd.at[:, pl.ds(mine, SLICE)], weights_peer)

    embed = [onehot(iota((WIDTH, PAIR), 1) == iota((WIDTH, PAIR), 0) + WIDTH * side) for side in range(2)]
    dense = iota((ROWS, 4 * PAD), 0)
    padded = dense + (PAD - SLOTS) * sum((dense >= SLOTS * n).astype(jnp.int32) for n in range(1, 4))
    pack = onehot(jnp.logical_and(padded == iota((ROWS, 4 * PAD), 1), dense < 4 * SLOTS))

    def holds(origin):
        r = lax.div(origin, 4)
        same = 1 - lax.rem(r + h, 2)
        source = origin + (1 - same) * (6 + 2 * lax.rem(origin, 2) - 2 * origin)
        return r, source - 4 * h

    def spot(n, kind, origin, first=0, count=ROWS):
        r, pair = holds(origin)
        return xg.at[n, kind, r, pl.ds(first, count), pl.ds(pl.multiple_of(pair * PAIR, PAIR), PAIR)]

    opposite = ((0, 96), (96, ROWS - 96))

    def repack(n):
        for side in range(2):
            for source in range(4):
                copies.arrived(arrived.at[4 * n + source, side], base + 2 * (4 * n + source) + side)
        wide = sum(dot(arrived[4 * n : 4 * n + 4, side].reshape(4 * PAD, WIDTH), embed[side]) for side in range(2))
        packed[n] = dot(pack, wide.astype(BF)).astype(BF)
        copy = copies.make(packed.at[n], block.at[n], mirror)
        here = pltpu.make_async_copy(packed.at[n], block.at[n], recv_sem.at[copies.recvs - 1])
        pl.when(pflip == 0)(here.start)
        pl.when(pflip == 1)(copy.start)
        to_self.append((pflip == 0, copy))
        return here

    class Gather:
        reach = {(0, 0): 4, (1, 0): 4, (0, 1): NEAR_RIGHT, (1, 1): NEAR_LEFT}

        def __init__(self, n):
            self.n = n
            self.moves = {}
            self.far = []
            self.here = pltpu.make_async_copy(block.at[n], spot(n, z, yq), local_sem.at[2 + n])
            self.here.start()
            self.push(0, 0, 1, block.at[n])
            self.push(1, 0, 1, block.at[n])
            self.swap = copies.go(block.at[n], spot(n, z, yq), across)

        def origin(self, way, step):
            return lax.rem(yq - step + 8, 8) if way == 0 else lax.rem(yq + step, 8)

        def push(self, way, kind, step, source=None):
            side = z if kind == 0 else 1 - z
            part = opposite[way] if step == 4 else (0, ROWS)
            ref = spot(self.n, side, self.origin(way, step - 1), *part)
            self.moves[way, kind, step] = copies.go(ref if source is None else source, ref, right if way == 0 else left)

        def swapped(self):
            self.swap.wait_recv()
            self.push(0, 1, 1)
            self.push(1, 1, 1)

        def own(self, step):
            for way in range(2):
                if step <= self.reach[way, 0]:
                    self.moves[way, 0, step].wait_recv()
                    if step < self.reach[way, 0]:
                        self.push(way, 0, step + 1)
                    if step > self.reach[way, 1]:
                        part = opposite[way] if step == 4 else (0, ROWS)
                        ref = spot(self.n, z, self.origin(way, step), *part)
                        self.far.append(copies.go(ref, ref, across))

        def other(self, step):
            for way in range(2):
                if step <= self.reach[way, 1]:
                    self.moves[way, 1, step].wait_recv()
                    if step < self.reach[way, 1]:
                        self.push(way, 1, step + 1)

        def finish(self):
            for copy in self.far:
                copy.wait_recv()
            self.here.wait()

    exchange = {}

    def forward(n):
        for which in range(3):
            data = xg[n, 1 if which == 2 else 0].reshape(2 * ROWS, HALF)
            if which < 2:
                value = dot(data, wgu[which])
            else:
                value = dot(data, wd[...], 1, 1)
            part[n, which] = value
            part_out[n, which] = value.astype(BF)
            exchange[n, which] = copies.go(part_out.at[n, which], part_in.at[n, which], rows_peer)
            yield

    def middle(n):
        for which in range(3):
            exchange[n, which].wait_recv()
        for r in range(2):
            span = pl.ds(r * ROWS, ROWS)
            gate, up, hidden = (part[n, w, span, :] + part_in[n, w, span, :].astype(F32) for w in range(3))
            sigma = jax.nn.sigmoid(gate)
            gate_grad = (hidden * up * sigma * (1.0 + gate * (1.0 - sigma))).astype(BF)
            up_grad = (hidden * gate * sigma).astype(BF)
            gu[n, r, :, :UNITS] = dot(pack, gate_grad, 0, 0).astype(BF)
            gu[n, r, :, UNITS:] = dot(pack, up_grad, 0, 0).astype(BF)
            yield

    back_base = copies.slots(EXPERTS)

    def backward(n):
        aways = (4, 3, 2, 1, -3, -2, -1, 0)
        swaps, moves = {}, {}

        def product(index):
            r, pair = holds(lax.rem(yq + aways[index] + 8, 8))
            span = pl.ds(pl.multiple_of(pair * PAIR, PAIR), PAIR)
            value = dot(gu[n, r, :, :UNITS], wgu[0, span, :], 1, 1)
            value = value + dot(gu[n, r, :, UNITS:], wgu[1, span, :], 1, 1)
            products[n, index] = value.astype(BF).reshape(2, 2 * PAD, PAIR)
            swaps[index] = copies.go(products.at[n, index, 1 - z], swapped.at[n, index], across)

        def mine(index):
            swaps[index].wait_recv()
            return products[n, index, z].astype(F32) + swapped[n, index].astype(F32)

        def link(index, way, first):
            value = mine(index)
            if not first:
                moves[index - 1].wait_recv()
                value = value + rows_in[n, index - 1].astype(F32)
            rows_out[n, index] = value.astype(BF)
            moves[index] = copies.go(rows_out.at[n, index], rows_in.at[n, index], way)

        for index in (0, 4, 1, 5, 2, 6, 3, 7):
            product(index)
        link(0, right, True)
        link(4, left, True)
        yield
        link(1, right, False)
        link(5, left, False)
        yield
        link(2, right, False)
        link(6, left, False)
        yield
        link(3, right, False)
        yield
        value = mine(7)
        for last in (6, 3):
            moves[last].wait_recv()
            value = value + rows_in[n, last].astype(F32)
        total = value.astype(BF)
        for side in range(2):
            back_out[n, side] = dot(total, embed[side], 1, 1).astype(BF).reshape(2, PAD, WIDTH)
        for turn in range(2):
            source = lax.rem(e + turn, 2)
            owner = 4 * n + 2 * z + source
            for side in range(2):
                slot = back_base + e
                target = {"expert": owner, "tensor": 2 * py + side, "dp": px}
                copy = copies.make(back_out.at[n, side, source], back.at[e], target, slot)
                stays = jnp.logical_and(jnp.logical_and(e == owner, z == side), pflip == 0)
                here = pltpu.make_async_copy(back_out.at[n, side, source], back.at[e], recv_sem.at[slot])
                pl.when(stays)(here.start)
                pl.when(jnp.logical_not(stays))(copy.start)
                to_self.append((stays, copy))
        yield

    def run(*work):
        for steps in work:
            for _ in steps:
                pass

    def advance(steps, times=1):
        for _ in range(times):
            next(steps, None)

    swap_a = repack(0)
    swap_b = repack(1)
    swap_a.wait()
    ga = Gather(0)
    swap_b.wait()
    gb = Gather(1)
    ga.own(1)
    ga.swapped()
    ga.own(2)
    ga.other(1)
    ga.own(3)
    gb.own(1)
    gb.swapped()
    ga.own(4)
    ga.other(2)
    gb.own(2)
    gb.other(1)
    ga.finish()
    own_gu.wait()
    own_d.wait()
    w1.wait_recv()
    w2.wait_recv()
    fa = forward(0)
    advance(fa)
    gb.own(3)
    gb.other(2)
    run(fa)
    gb.own(4)
    gb.finish()
    run(forward(1))
    run(middle(0))
    ba = backward(0)
    advance(ba, 2)
    run(middle(1))
    bb = backward(1)
    for _ in range(3):
        advance(bb)
        advance(ba)
    run(bb)
    for other in range(EXPERTS):
        copies.arrived(back.at[other], back_base + other)

    returned = back[...].reshape(EXPERTS * PAD, WIDTH)
    gates = gates_ref[...]
    diagonal = iota((count, count), 0) == iota((count, count), 1)
    total = jnp.zeros((count, WIDTH), F32)
    for k in range(2):
        gate = jnp.sum(jnp.where(diagonal, gates[k : k + 1, :], 0.0), axis=1, keepdims=True)
        total = total + gate * dot(picks[k].astype(BF), returned, 0, 0)
    result_ref[...] = total.astype(BF)

    for copy in copies.pending:
        copy.wait_send()
    for stays, copy in to_self:
        pl.when(jnp.logical_not(stays))(copy.wait_send)
    assert copies.sends <= SENDS and copies.recvs <= RECVS


def body(tokens, out_grad, gates, expert_ids, w_gate_up, w_down):
    vmem = pl.BlockSpec(memory_space=pltpu.VMEM)
    hbm = pl.BlockSpec(memory_space=pl.ANY)
    return pl.pallas_call(
        kernel,
        out_shape=jax.ShapeDtypeStruct(tokens.shape, BF),
        in_specs=[hbm] * 6,
        out_specs=vmem,
        scratch_shapes=[
            pltpu.VMEM((2, EXPERTS, PAD, WIDTH), BF),
            pltpu.VMEM((EXPERTS, 2, PAD, WIDTH), BF),
            pltpu.VMEM((2, ROWS, PAIR), BF),
            pltpu.VMEM((2, ROWS, PAIR), BF),
            pltpu.VMEM((2, 2, 2, ROWS, HALF), BF),
            pltpu.VMEM((2, HALF, UNITS), BF),
            pltpu.VMEM((UNITS, HALF), BF),
            pltpu.VMEM((2, 3, 2 * ROWS, UNITS), F32),
            pltpu.VMEM((2, 3, 2 * ROWS, UNITS), BF),
            pltpu.VMEM((2, 3, 2 * ROWS, UNITS), BF),
            pltpu.VMEM((2, 2, 4 * PAD, 2 * UNITS), BF),
            pltpu.VMEM((2, 8, 2, 2 * PAD, PAIR), BF),
            pltpu.VMEM((2, 8, 2 * PAD, PAIR), BF),
            pltpu.VMEM((2, 7, 2 * PAD, PAIR), BF),
            pltpu.VMEM((2, 7, 2 * PAD, PAIR), BF),
            pltpu.VMEM((2, 2, 2, PAD, WIDTH), BF),
            pltpu.VMEM((EXPERTS, PAD, WIDTH), BF),
            pltpu.VMEM(tokens.shape, BF),
            pltpu.VMEM(tokens.shape, BF),
            pltpu.VMEM(gates.shape[::-1], F32),
            pltpu.VMEM(gates.shape[::-1], jnp.int32),
            pltpu.SemaphoreType.DMA((SENDS,)),
            pltpu.SemaphoreType.DMA((RECVS,)),
            pltpu.SemaphoreType.DMA((8,)),
        ],
        compiler_params=pltpu.CompilerParams(
            collective_id=0, has_side_effects=True, vmem_limit_bytes=56 * 1024 * 1024
        ),
    )(tokens, out_grad, gates.T, expert_ids.T, w_gate_up, w_down)


def solution(mesh):
    return jax.shard_map(
        body,
        mesh=mesh,
        in_specs=(
            P(("expert", "dp"), "tensor"),
            P(("expert", "dp"), "tensor"),
            P(("expert", "dp"), None),
            P(("expert", "dp"), None),
            P("expert", None, "dp", "tensor"),
            P("expert", "tensor", "dp"),
        ),
        out_specs=P(("expert", "dp"), "tensor"),
        check_vma=False,
    )
```

```python
import jax
import jax.numpy as jnp
from jax import lax
from jax.experimental import pallas as pl
from jax.experimental.pallas import tpu as pltpu
from jax.sharding import PartitionSpec as P

MESH = pl.DeviceIdType.MESH
EXPERTS = 8
SLOTS = 42
PAD = 48
WIDTH = 192
PAIR = 384
ROWS = 176
HALF = 1536
SLICE = 768
UNITS = 512
NEAR_RIGHT = 1
NEAR_LEFT = 1
ORDER = (4, 5, 3, 2, 6, 1, 7, 0)
BF = jnp.bfloat16
F32 = jnp.float32


def iota(shape, dim):
    return lax.broadcasted_iota(jnp.int32, shape, dim)


def dot(a, b, ca=1, cb=0):
    return lax.dot_general(a, b, (((ca,), (cb,)), ((), ())), preferred_element_type=F32)


def onehot(mask):
    return mask.astype(F32).astype(BF)


class Copies:
    def __init__(self, send, recv):
        self.send, self.recv = send, recv
        self.sends, self.recvs = 0, 0
        self.pending = []

    def slots(self, count):
        first = self.recvs
        self.recvs += count
        return first

    def make(self, src, dst, device, slot=None):
        if slot is None:
            slot = self.slots(1)
        copy = pltpu.make_async_remote_copy(
            src_ref=src,
            dst_ref=dst,
            send_sem=self.send.at[self.sends],
            recv_sem=self.recv.at[slot],
            device_id=device,
            device_id_type=MESH,
        )
        self.sends += 1
        return copy

    def go(self, src, dst, device, slot=None):
        copy = self.make(src, dst, device, slot)
        copy.start()
        self.pending.append(copy)
        return copy

    def arrived(self, ref, slot):
        pltpu.make_async_copy(ref, ref, self.recv.at[slot]).wait()


SENDS = 160
RECVS = 160


def kernel(
    tokens_hbm, grads_hbm, gates_hbm, ids_hbm, wgu_hbm, wd_hbm,
    result_ref,
    outgoing, arrived, packed, block, xg, wgu, wd, part, part_out, part_in, gu, products, swapped,
    rows_out, rows_in, back_out, back, tokens_ref, grads_ref, gates_ref, ids_ref, send_sem, recv_sem, local_sem,
):
    e = lax.axis_index("expert")
    t = lax.axis_index("tensor")
    x = lax.axis_index("dp")
    c = lax.rem(e, 2)
    y, z = lax.div(t, 2), lax.rem(t, 2)
    yq = lax.rem(y - 2 * c + 8, 8)
    xq = lax.rem(x - c + 4, 4)
    h = lax.div(xq, 2)
    odd = lax.rem(xq, 2)

    right = {"tensor": 2 * lax.rem(y + 1, 8) + z}
    left = {"tensor": 2 * lax.rem(y + 7, 8) + z}
    across = {"tensor": 2 * y + (1 - z)}
    weights_peer = {"dp": lax.rem(xq + 1 - 2 * odd + c, 4)}
    rows_peer = {"dp": lax.rem(3 - xq + c, 4)}

    def place(core):
        xs = lax.rem(x - core + 4, 4)
        ys = lax.rem(y - 2 * core + 8, 8)
        flip = lax.rem(lax.div(xs, 2) + lax.div(ys, 4), 2)
        x2 = xs + flip * (3 - 2 * xs)
        y2 = ys + flip * (6 + 2 * lax.rem(ys, 2) - 2 * ys)
        return lax.rem(x2 + core, 4), lax.rem(y2 + 2 * core, 8), flip

    px, py, pflip = place(c)
    mirror = {"tensor": 2 * py + z, "dp": px}
    copies = Copies(send_sem, recv_sem)

    barrier = pltpu.get_barrier_semaphore()
    signals = 0
    for turn in ORDER:
        other = lax.rem(e + turn, EXPERTS)
        for side in range(2):
            pl.semaphore_signal(
                barrier, inc=1, device_id={"expert": other, "tensor": 2 * y + side}, device_id_type=MESH
            )
            signals += 1
    for peer in (right, left, across, weights_peer, rows_peer, mirror):
        pl.semaphore_signal(barrier, inc=1, device_id=peer, device_id_type=MESH)
        signals += 1

    loads = [
        pltpu.make_async_copy(source, target, local_sem.at[4 + i])
        for i, (source, target) in enumerate(
            ((ids_hbm, ids_ref), (tokens_hbm, tokens_ref), (grads_hbm, grads_ref), (gates_hbm, gates_ref))
        )
    ]
    for load in loads:
        load.start()
    mine = pl.multiple_of(odd * SLICE, SLICE)
    own_gu = pltpu.make_async_copy(wgu_hbm.at[0], wgu.at[:, pl.ds(mine, SLICE), :], local_sem.at[0])
    own_d = pltpu.make_async_copy(wd_hbm.at[0], wd.at[:, pl.ds(mine, SLICE)], local_sem.at[1])
    own_gu.start()
    own_d.start()

    for load in loads:
        load.wait()
    ids = ids_ref[...]
    count = ids.shape[1]
    lines = iota((EXPERTS, count), 0)
    chosen = [(ids[k : k + 1, :] == lines).astype(F32) for k in range(2)]
    earlier = onehot(iota((count, count), 0) < iota((count, count), 1))
    before = dot((chosen[0] + chosen[1]).astype(BF), earlier)
    slot_of = before + (lines * PAD).astype(F32)
    slot_lines = iota((EXPERTS * PAD, count), 0)
    picks = []
    for k in range(2):
        target = jnp.sum(chosen[k] * slot_of, axis=0, keepdims=True).astype(jnp.int32)
        picks.append((target == slot_lines).astype(F32))
    select = (picks[0] + picks[1]).astype(BF)
    for kind, source in enumerate((tokens_ref, grads_ref)):
        chosen_rows = dot(select, source[...]).astype(BF)
        outgoing[kind] = chosen_rows.reshape(EXPERTS, PAD, WIDTH)

    pl.semaphore_wait(barrier, signals)

    base = copies.slots(2 * EXPERTS)
    to_self = []
    for turn in ORDER:
        other = lax.rem(e + turn, EXPERTS)
        for kind in range(2):
            target = {"expert": other, "tensor": 2 * y + kind}
            slot = base + 2 * e + z
            copy = copies.make(outgoing.at[kind, other], arrived.at[e, z], target, slot)
            if turn:
                copy.start()
                copies.pending.append(copy)
                continue
            stays = z == kind
            here = pltpu.make_async_copy(outgoing.at[kind, other], arrived.at[e, z], recv_sem.at[slot])
            pl.when(stays)(here.start)
            pl.when(jnp.logical_not(stays))(copy.start)
            to_self.append((stays, copy))

    w1 = copies.go(wgu_hbm.at[0], wgu.at[:, pl.ds(mine, SLICE), :], weights_peer)
    w2 = copies.go(wd_hbm.at[0], wd.at[:, pl.ds(mine, SLICE)], weights_peer)

    embed = [onehot(iota((WIDTH, PAIR), 1) == iota((WIDTH, PAIR), 0) + WIDTH * side) for side in range(2)]
    dense = iota((ROWS, 4 * PAD), 0)
    padded = dense + (PAD - SLOTS) * sum((dense >= SLOTS * n).astype(jnp.int32) for n in range(1, 4))
    pack = onehot(jnp.logical_and(padded == iota((ROWS, 4 * PAD), 1), dense < 4 * SLOTS))

    def holds(origin):
        r = lax.div(origin, 4)
        same = 1 - lax.rem(r + h, 2)
        source = origin + (1 - same) * (6 + 2 * lax.rem(origin, 2) - 2 * origin)
        return r, source - 4 * h

    def spot(n, kind, origin, first=0, count=ROWS):
        r, pair = holds(origin)
        return xg.at[n, kind, r, pl.ds(first, count), pl.ds(pl.multiple_of(pair * PAIR, PAIR), PAIR)]

    opposite = ((0, 96), (96, ROWS - 96))

    def repack(n):
        for side in range(2):
            for source in range(4):
                copies.arrived(arrived.at[4 * n + source, side], base + 2 * (4 * n + source) + side)
        wide = sum(dot(arrived[4 * n : 4 * n + 4, side].reshape(4 * PAD, WIDTH), embed[side]) for side in range(2))
        packed[n] = dot(pack, wide.astype(BF)).astype(BF)
        copy = copies.make(packed.at[n], block.at[n], mirror)
        here = pltpu.make_async_copy(packed.at[n], block.at[n], recv_sem.at[copies.recvs - 1])
        pl.when(pflip == 0)(here.start)
        pl.when(pflip == 1)(copy.start)
        to_self.append((pflip == 0, copy))
        return here

    class Gather:
        reach = {(0, 0): 4, (1, 0): 4, (0, 1): NEAR_RIGHT, (1, 1): NEAR_LEFT}

        def __init__(self, n):
            self.n = n
            self.moves = {}
            self.far = []
            self.here = pltpu.make_async_copy(block.at[n], spot(n, z, yq), local_sem.at[2 + n])
            self.here.start()
            self.push(0, 0, 1, block.at[n])
            self.push(1, 0, 1, block.at[n])
            self.swap = copies.go(block.at[n], spot(n, z, yq), across)

        def origin(self, way, step):
            return lax.rem(yq - step + 8, 8) if way == 0 else lax.rem(yq + step, 8)

        def push(self, way, kind, step, source=None):
            side = z if kind == 0 else 1 - z
            part = opposite[way] if step == 4 else (0, ROWS)
            ref = spot(self.n, side, self.origin(way, step - 1), *part)
            self.moves[way, kind, step] = copies.go(ref if source is None else source, ref, right if way == 0 else left)

        def swapped(self):
            self.swap.wait_recv()
            self.push(0, 1, 1)
            self.push(1, 1, 1)

        def own(self, step):
            for way in range(2):
                if step <= self.reach[way, 0]:
                    self.moves[way, 0, step].wait_recv()
                    if step < self.reach[way, 0]:
                        self.push(way, 0, step + 1)
                    if step > self.reach[way, 1]:
                        part = opposite[way] if step == 4 else (0, ROWS)
                        ref = spot(self.n, z, self.origin(way, step), *part)
                        self.far.append(copies.go(ref, ref, across))

        def other(self, step):
            for way in range(2):
                if step <= self.reach[way, 1]:
                    self.moves[way, 1, step].wait_recv()
                    if step < self.reach[way, 1]:
                        self.push(way, 1, step + 1)

        def finish(self):
            for copy in self.far:
                copy.wait_recv()
            self.here.wait()

    exchange = {}

    def forward(n):
        for which in range(3):
            data = xg[n, 1 if which == 2 else 0].reshape(2 * ROWS, HALF)
            if which < 2:
                value = dot(data, wgu[which])
            else:
                value = dot(data, wd[...], 1, 1)
            part[n, which] = value
            part_out[n, which] = value.astype(BF)
            exchange[n, which] = copies.go(part_out.at[n, which], part_in.at[n, which], rows_peer)
            yield

    def middle(n):
        for which in range(3):
            exchange[n, which].wait_recv()
        for r in range(2):
            span = pl.ds(r * ROWS, ROWS)
            gate, up, hidden = (part[n, w, span, :] + part_in[n, w, span, :].astype(F32) for w in range(3))
            sigma = jax.nn.sigmoid(gate)
            gate_grad = (hidden * up * sigma * (1.0 + gate * (1.0 - sigma))).astype(BF)
            up_grad = (hidden * gate * sigma).astype(BF)
            gu[n, r, :, :UNITS] = dot(pack, gate_grad, 0, 0).astype(BF)
            gu[n, r, :, UNITS:] = dot(pack, up_grad, 0, 0).astype(BF)
            yield

    back_base = copies.slots(EXPERTS)

    def backward(n):
        aways = (4, 3, 2, 1, -3, -2, -1, 0)
        swaps, moves = {}, {}

        def product(index):
            r, pair = holds(lax.rem(yq + aways[index] + 8, 8))
            span = pl.ds(pl.multiple_of(pair * PAIR, PAIR), PAIR)
            value = dot(gu[n, r, :, :UNITS], wgu[0, span, :], 1, 1)
            value = value + dot(gu[n, r, :, UNITS:], wgu[1, span, :], 1, 1)
            products[n, index] = value.astype(BF).reshape(2, 2 * PAD, PAIR)
            swaps[index] = copies.go(products.at[n, index, 1 - z], swapped.at[n, index], across)

        def mine(index):
            swaps[index].wait_recv()
            return products[n, index, z].astype(F32) + swapped[n, index].astype(F32)

        def link(index, way, first):
            value = mine(index)
            if not first:
                moves[index - 1].wait_recv()
                value = value + rows_in[n, index - 1].astype(F32)
            rows_out[n, index] = value.astype(BF)
            moves[index] = copies.go(rows_out.at[n, index], rows_in.at[n, index], way)

        for index in (0, 4, 1, 5, 2, 6, 3, 7):
            product(index)
        link(0, right, True)
        link(4, left, True)
        yield
        link(1, right, False)
        link(5, left, False)
        yield
        link(2, right, False)
        link(6, left, False)
        yield
        link(3, right, False)
        yield
        value = mine(7)
        for last in (6, 3):
            moves[last].wait_recv()
            value = value + rows_in[n, last].astype(F32)
        total = value.astype(BF)
        for side in range(2):
            back_out[n, side] = dot(total, embed[side], 1, 1).astype(BF).reshape(2, PAD, WIDTH)
        for turn in range(2):
            source = lax.rem(e + turn, 2)
            owner = 4 * n + 2 * z + source
            for side in range(2):
                slot = back_base + e
                target = {"expert": owner, "tensor": 2 * py + side, "dp": px}
                copy = copies.make(back_out.at[n, side, source], back.at[e], target, slot)
                stays = jnp.logical_and(jnp.logical_and(e == owner, z == side), pflip == 0)
                here = pltpu.make_async_copy(back_out.at[n, side, source], back.at[e], recv_sem.at[slot])
                pl.when(stays)(here.start)
                pl.when(jnp.logical_not(stays))(copy.start)
                to_self.append((stays, copy))
        yield

    def run(*work):
        for steps in work:
            for _ in steps:
                pass

    def advance(steps, times=1):
        for _ in range(times):
            next(steps, None)

    swap_a = repack(0)
    swap_b = repack(1)
    swap_a.wait()
    ga = Gather(0)
    swap_b.wait()
    gb = Gather(1)
    ga.own(1)
    ga.swapped()
    ga.own(2)
    ga.other(1)
    ga.own(3)
    gb.own(1)
    gb.swapped()
    ga.own(4)
    ga.other(2)
    gb.own(2)
    gb.other(1)
    ga.finish()
    own_gu.wait()
    own_d.wait()
    w1.wait_recv()
    w2.wait_recv()
    fa = forward(0)
    advance(fa)
    gb.own(3)
    gb.other(2)
    run(fa)
    gb.own(4)
    gb.finish()
    run(forward(1))
    run(middle(0))
    ba = backward(0)
    advance(ba, 2)
    run(middle(1))
    bb = backward(1)
    for _ in range(3):
        advance(bb)
        advance(ba)
    run(bb)
    for other in range(EXPERTS):
        copies.arrived(back.at[other], back_base + other)

    returned = back[...].reshape(EXPERTS * PAD, WIDTH)
    gates = gates_ref[...]
    diagonal = iota((count, count), 0) == iota((count, count), 1)
    total = jnp.zeros((count, WIDTH), F32)
    for k in range(2):
        gate = jnp.sum(jnp.where(diagonal, gates[k : k + 1, :], 0.0), axis=1, keepdims=True)
        total = total + gate * dot(picks[k].astype(BF), returned, 0, 0)
    result_ref[...] = total.astype(BF)

    for copy in copies.pending:
        copy.wait_send()
    for stays, copy in to_self:
        pl.when(jnp.logical_not(stays))(copy.wait_send)
    assert copies.sends <= SENDS and copies.recvs <= RECVS


def body(tokens, out_grad, gates, expert_ids, w_gate_up, w_down):
    vmem = pl.BlockSpec(memory_space=pltpu.VMEM)
    hbm = pl.BlockSpec(memory_space=pl.ANY)
    return pl.pallas_call(
        kernel,
        out_shape=jax.ShapeDtypeStruct(tokens.shape, BF),
        in_specs=[hbm] * 6,
        out_specs=vmem,
        scratch_shapes=[
            pltpu.VMEM((2, EXPERTS, PAD, WIDTH), BF),
            pltpu.VMEM((EXPERTS, 2, PAD, WIDTH), BF),
            pltpu.VMEM((2, ROWS, PAIR), BF),
            pltpu.VMEM((2, ROWS, PAIR), BF),
            pltpu.VMEM((2, 2, 2, ROWS, HALF), BF),
            pltpu.VMEM((2, HALF, UNITS), BF),
            pltpu.VMEM((UNITS, HALF), BF),
            pltpu.VMEM((2, 3, 2 * ROWS, UNITS), F32),
            pltpu.VMEM((2, 3, 2 * ROWS, UNITS), BF),
            pltpu.VMEM((2, 3, 2 * ROWS, UNITS), BF),
            pltpu.VMEM((2, 2, 4 * PAD, 2 * UNITS), BF),
            pltpu.VMEM((2, 8, 2, 2 * PAD, PAIR), BF),
            pltpu.VMEM((2, 8, 2 * PAD, PAIR), BF),
            pltpu.VMEM((2, 7, 2 * PAD, PAIR), BF),
            pltpu.VMEM((2, 7, 2 * PAD, PAIR), BF),
            pltpu.VMEM((2, 2, 2, PAD, WIDTH), BF),
            pltpu.VMEM((EXPERTS, PAD, WIDTH), BF),
            pltpu.VMEM(tokens.shape, BF),
            pltpu.VMEM(tokens.shape, BF),
            pltpu.VMEM(gates.shape[::-1], F32),
            pltpu.VMEM(gates.shape[::-1], jnp.int32),
            pltpu.SemaphoreType.DMA((SENDS,)),
            pltpu.SemaphoreType.DMA((RECVS,)),
            pltpu.SemaphoreType.DMA((8,)),
        ],
        compiler_params=pltpu.CompilerParams(
            collective_id=0, has_side_effects=True, vmem_limit_bytes=56 * 1024 * 1024
        ),
    )(tokens, out_grad, gates.T, expert_ids.T, w_gate_up, w_down)


def solution(mesh):
    return jax.shard_map(
        body,
        mesh=mesh,
        in_specs=(
            P(("expert", "dp"), "tensor"),
            P(("expert", "dp"), "tensor"),
            P(("expert", "dp"), None),
            P(("expert", "dp"), None),
            P("expert", None, "dp", "tensor"),
            P("expert", "tensor", "dp"),
        ),
        out_specs=P(("expert", "dp"), "tensor"),
        check_vma=False,
    )
```
